32 devices in a mesh: groups: 2 (over y), dp: 2 (over x), ctx: 4 (over z), tp: 2 (over core).
Axes of the slice: x: 2, y: 2, z: 4, core: 2. Of those that a mesh axis runs over, the one named last changes fastest.
Arguments:
- queries: bfloat16 [4, 1024, 2048], P(('groups', 'dp'), 'ctx', 'tp'), parts along dimension 0, may hold values from -20 to 20
- keyvals: bfloat16 [4, 1024, 2, 512], P(('groups', 'dp'), 'ctx', None, 'tp'), parts along dimension 0, may hold values from -20 to 20
- doc_ids: int32 [4, 1024], P(('groups', 'dp'), 'ctx'), parts along dimension 0, may hold values from 0 to 64, as said below
- plan: int32 [4, 4], P(('groups', 'dp')), parts along dimension 0, may hold values from 0 to 3, as said below
- lengths: int32 [4, 8], P(('groups', 'dp')), parts along dimension 0, may hold values from 1 to 512, 1024 in all within a row
- out_weight: bfloat16 [2048, 4096], P('tp', 'dp'), may hold values from -0.5 to 0.5
Outputs:
- mixed_out: bfloat16 [4, 1024, 4096], P(('groups', 'dp'), 'ctx', 'tp'), parts along dimension 0
The draws below stay inside these ranges and needn't reach their ends.
There are 2 independent parts, one for each index of `groups`. The reference program is written for one: setup_inputs(seed, part) draws one part's arguments, and reference() takes and returns one part's arrays. A program takes and returns all parts, laid end to end along the dimension named above; an argument that names none is the same for every part. Nothing has to cross between parts.
Inputs may be any that keep to these rules, and one draw needn't show every extreme that they name: `lengths`: each row sums to 1024. `plan`: each row names every block of its request group once. `doc_ids`: 0 marks tokens that see every earlier token of their request.
All inputs are finite; a program needn't handle non-finite values.
Results may differ from the reference program's by a relative error of at most 0.0061.
Values may be sent and summed in bfloat16 or wider, within the bound.
A program may use at most 128 MiB of HBM per device.

```python
import math
import jax
import jax.numpy as jnp
import numpy as np
from jax import lax

D = 4096
HEADS = 16
KVH = 4
HD = 128
TOK_DEV = 256
REQS = 8
ROWS = 2
BLOCKS = 4
SEQ = 1024
HGROUP = 8
N_TP = 2


def plan_docs(key):
    plan_keys = jax.random.split(jax.random.fold_in(key, 7), ROWS)
    placing = jax.vmap(lambda sub_key: jax.random.permutation(sub_key, BLOCKS))(plan_keys).astype(jnp.int32)
    cut_key, kind_key = jax.random.split(jax.random.fold_in(key, 8))
    cuts = (jax.random.randint(cut_key, (ROWS, SEQ), 0, max(SEQ // 16, 2)) == 0).astype(jnp.int32)
    segment = jnp.cumsum(cuts, axis=1).astype(jnp.int32)
    kinds = jax.random.randint(kind_key, (ROWS, SEQ + 1), 0, 4)
    labels = jnp.where(jnp.take_along_axis(kinds, segment, axis=1) == 0, 0, segment % 63 + 1).astype(jnp.int32)
    where_seq = jnp.arange(SEQ, dtype=jnp.int32)[None, :]
    labels = jnp.where(where_seq == SEQ - 1, 64, labels)
    labels = jnp.where(where_seq == 0, 0, labels).astype(jnp.int32)
    blocked = labels.reshape(ROWS, BLOCKS, TOK_DEV)
    in_slots = jnp.take_along_axis(blocked, placing[:, :, None], axis=1).reshape(ROWS, SEQ)
    return (placing, in_slots.astype(jnp.int32))


def float_fields(key):
    base_key = jax.random.fold_in(key, 29)
    query_key, key_key, value_key = jax.random.split(base_key, 3)
    query_rows = jnp.clip(jax.random.normal(query_key, (ROWS, SEQ, HEADS, HD), jnp.float32), -4.0, 4.0)
    key_rows = jnp.clip(jax.random.normal(key_key, (ROWS, SEQ, KVH, HD), jnp.float32), -4.0, 4.0)
    value_rows = jnp.clip(jax.random.normal(value_key, (ROWS, SEQ, KVH, HD), jnp.float32), -4.0, 4.0)
    query_flat = query_rows.reshape(ROWS, SEQ, HEADS * HD)
    pair = jnp.stack([key_rows.reshape(ROWS, SEQ, KVH * HD), value_rows.reshape(ROWS, SEQ, KVH * HD)], axis=2)
    return (query_flat, pair)


def draw_queries(key, part):
    query_flat, pair = float_fields(key)
    return query_flat.astype(jnp.bfloat16)


def draw_keyvals(key, part):
    query_flat, pair = float_fields(key)
    return pair.astype(jnp.bfloat16)


def draw_doc_ids(key, part):
    placing, in_slots = plan_docs(key)
    return in_slots


def draw_plan(key, part):
    placing, in_slots = plan_docs(key)
    return placing


def block_levels(own_key, extent, pieces, low, high):
    level = 1.0
    for axis_at, shards_of in pieces:
        heights = jax.random.uniform(jax.random.fold_in(jax.random.fold_in(own_key, 6), axis_at), (shards_of,), jnp.float32, low / len(pieces), high / len(pieces))
        level = level * jnp.repeat(jnp.exp(heights), extent[axis_at] // shards_of).reshape((-1,) + (1,) * (len(extent) - 1 - axis_at))
    return level


def split_up(number_of, total, limit, lean):
    weights = [(1 << 20) // math.isqrt(grade ** lean) + 1 for grade in range(2, number_of + 1)]
    rest, holding = total - limit - (number_of - 1), [1] * (number_of - 1)
    while rest > 0:
        candidates = [i for i in range(number_of - 1) if holding[i] < limit]
        mass, budget = sum([weights[i] for i in candidates]), rest
        for i in candidates:
            extra = min(limit - holding[i], max(1, budget * weights[i] // mass), rest)
            holding[i] = holding[i] + extra
            rest = rest - extra
    return np.array([limit] + holding)


def uneven_parts(stream_key, amount, total, reach, slope):
    if amount == 2:
        one = jax.random.randint(stream_key, (), max(1, total - reach), min(reach, total - 1) + 1)
        return jnp.stack([one, total - one])
    tallies = jnp.asarray(split_up(amount, total, reach, slope), jnp.int32)
    couples = (amount - 1) // 2
    giver, taker = tallies[1:1 + 2 * couples:2], tallies[2:2 + 2 * couples:2]
    room = jnp.minimum(giver - 1, reach - taker)
    moved = jax.random.randint(jax.random.fold_in(stream_key, 1), (couples,), 0, 1 << 20) % (room + 1)
    tallies = tallies.at[1:1 + 2 * couples:2].set(giver - moved).at[2:2 + 2 * couples:2].set(taker + moved)
    return tallies[jax.random.permutation(jax.random.fold_in(stream_key, 2), amount)]


def noise(rng, shape, scale, bound, cuts=(), kind=jnp.bfloat16):
    loudness = block_levels(rng, shape, cuts, -0.22, 0.18) if cuts else 1.0
    values = jax.random.normal(rng, shape, jnp.float32) * scale * loudness
    return jnp.minimum(jnp.maximum(values, -bound), bound).astype(kind)


def setup_inputs(seed: int = 0, part: int = 0) -> dict:
    streams_of = jax.random.split(jax.random.key(seed), 7)
    part_keys = jax.random.split(jax.random.fold_in(streams_of[6], part), 7)
    queries = draw_queries(jax.random.fold_in(jax.random.fold_in(streams_of[6], part), 71), part)
    keyvals = draw_keyvals(jax.random.fold_in(jax.random.fold_in(streams_of[6], part), 71), part)
    doc_ids = draw_doc_ids(jax.random.fold_in(jax.random.fold_in(streams_of[6], part), 71), part)
    plan = draw_plan(jax.random.fold_in(jax.random.fold_in(streams_of[6], part), 71), part)
    lengths = jax.vmap(lambda own: uneven_parts(own, REQS, SEQ, SEQ // 2, 2))(jax.random.split(part_keys[4], ROWS)).reshape((ROWS, REQS)).astype(jnp.int32)
    out_weight = noise(streams_of[5], (HEADS * HD, D), (HEADS * HD // 16) ** -0.5, 0.5, ((0, 2), (1, 2)))
    return dict(queries=queries, keyvals=keyvals, doc_ids=doc_ids, plan=plan, lengths=lengths, out_weight=out_weight)


def request_of(positions, request_ends):
    return jnp.sum((request_ends[None, :] <= positions[:, None]).astype(jnp.int32), axis=1)


def attend_row(query_row, kv_row, docs_row, placing, lengths_row):
    offsets = jnp.arange(TOK_DEV, dtype=jnp.int32)
    positions = (placing[:, None] * TOK_DEV + offsets[None, :]).reshape(SEQ).astype(jnp.int32)
    requests = request_of(positions, jnp.cumsum(lengths_row).astype(jnp.int32))
    group_size = HEADS // KVH
    key_all = jnp.repeat(kv_row[:, 0].reshape(SEQ, KVH, HD), group_size, axis=1).astype(jnp.float32)
    value_all = jnp.repeat(kv_row[:, 1].reshape(SEQ, KVH, HD), group_size, axis=1).astype(jnp.float32)
    query_all = query_row.reshape(SEQ, HEADS, HD).astype(jnp.float32)
    width = 512 if SEQ % 512 == 0 else SEQ

    def attend_block(block_index):
        first_row = (block_index * width).astype(jnp.int32)
        query_block = lax.dynamic_slice_in_dim(query_all, first_row, width, 0)
        pos_block = lax.dynamic_slice_in_dim(positions, first_row, width, 0)
        req_block = lax.dynamic_slice_in_dim(requests, first_row, width, 0)
        doc_block = lax.dynamic_slice_in_dim(docs_row, first_row, width, 0)
        allowed = (req_block[:, None] == requests[None, :]) & (positions[None, :] <= pos_block[:, None])
        allowed = allowed & ((doc_block[:, None] == docs_row[None, :]) | (doc_block[:, None] == 0))
        scores = jnp.einsum("qhd,khd->hqk", query_block, key_all, precision=lax.Precision.HIGHEST) * (HD ** -0.5)
        scores = jnp.where(allowed[None], scores, -1e30)
        row_max = jnp.max(scores, axis=2)
        probs = jnp.where(allowed[None], jnp.exp(scores - row_max[:, :, None]), 0.0)
        denominator = jnp.sum(probs, axis=2)
        rounded = lax.optimization_barrier(probs.astype(jnp.bfloat16)).astype(jnp.float32)
        summed = jnp.einsum("hqk,khd->qhd", rounded, value_all, precision=lax.Precision.HIGHEST)
        result = summed / jnp.transpose(denominator)[:, :, None]
        return result.reshape(width, HEADS * HD).astype(jnp.bfloat16)

    blocks = lax.map(attend_block, jnp.arange(SEQ // width, dtype=jnp.int32))
    return blocks.reshape(SEQ, HEADS * HD)


def reference(queries, keyvals, doc_ids, plan, lengths, out_weight):
    attended = jnp.stack([attend_row(queries[row], keyvals[row], doc_ids[row], plan[row], lengths[row]) for row in range(ROWS)])
    flat = attended.reshape(ROWS * SEQ, HEADS * HD)
    span = HGROUP * HD
    summed = jnp.zeros((ROWS * SEQ, D), jnp.float32)
    for group in range(N_TP):
        partial_value = jnp.dot(flat[:, group * span:(group + 1) * span], out_weight[group * span:(group + 1) * span], preferred_element_type=jnp.float32)
        summed = summed + lax.optimization_barrier(partial_value.astype(jnp.bfloat16)).astype(jnp.float32)
    return summed.astype(jnp.bfloat16).reshape(ROWS, SEQ, D)
```

```python
import functools
import math

import jax
import jax.numpy as jnp
from jax import lax
from jax.experimental import pallas as pl
from jax.experimental.pallas import tpu as pltpu
from jax.sharding import PartitionSpec as P

HD = 128
LANES = 128
MESH = pl.DeviceIdType.MESH
NEG = -1e30


def wide(x, width):
    return jnp.concatenate([x] * (width // LANES), axis=1) if width > LANES else x


def kernel(
    cfg,
    plan_ref,
    len_ref,
    q_ref,
    kv_ref,
    doc_ref,
    w_hbm,
    out_hbm,
    kvbuf,
    dbuf,
    lo_buf,
    qd_buf,
    m_buf,
    l_buf,
    acc_buf,
    att,
    w_buf,
    part,
    prec,
    fin,
    w_sem,
    kv_send,
    kv_recv,
    doc_send,
    doc_recv,
    att_send,
    att_recv,
    part_send,
    part_recv,
    fin_send,
    fin_recv,
    loc_sem,
):
    n, rows, cores, tok, kvh, gsz, reqs, cols, halves, chunks = cfg
    me = lax.axis_index("ctx")
    d = lax.axis_index("dp")
    t = lax.axis_index("tp")
    other = 1 - t
    hrows = tok // halves
    ccols = cols // chunks
    gcols = gsz * HD
    per_half = rows // cores
    scale = HD ** (-0.5) * math.log2(math.e)

    w_copy = pltpu.make_async_copy(w_hbm, w_buf, w_sem)
    w_copy.start()

    barrier = pltpu.get_barrier_semaphore()

    @pl.when(me > 0)
    def _():
        pl.semaphore_signal(barrier, inc=1, device_id={"ctx": me - 1}, device_id_type=MESH)

    @pl.when(me < n - 1)
    def _():
        pl.semaphore_signal(barrier, inc=1, device_id={"ctx": me + 1}, device_id_type=MESH)

    for k in range(rows):
        for c in range(cores):
            if k == 0 and c == 0:
                continue
            pl.semaphore_signal(
                barrier,
                inc=1,
                device_id={"dp": lax.rem(d + k, rows), "tp": lax.rem(t + c, cores)},
                device_id_type=MESH,
            )
    ends = (me > 0).astype(jnp.int32) + (me < n - 1).astype(jnp.int32)
    pl.semaphore_wait(barrier, rows * cores - 1 + ends)

    def kv_copy(way, step, g, src, block):
        return pltpu.make_async_remote_copy(
            src_ref=src,
            dst_ref=kvbuf.at[block, g],
            send_sem=kv_send.at[way, step, g],
            recv_sem=kv_recv.at[way, step, g],
            device_id={"ctx": me + 1 if way == 0 else me - 1},
            device_id_type=MESH,
        )

    def doc_copy(way, step, src, block):
        return pltpu.make_async_remote_copy(
            src_ref=src,
            dst_ref=dbuf.at[block],
            send_sem=doc_send.at[way, step],
            recv_sem=doc_recv.at[way, step],
            device_id={"ctx": me + 1 if way == 0 else me - 1},
            device_id_type=MESH,
        )

    can = (me < n - 1, me > 0)
    for way in range(2):

        @pl.when(can[way])
        def _(way=way):
            doc_copy(way, 0, doc_ref, me).start()
            for g in range(kvh):
                kv_copy(way, 0, g, kv_ref.at[g], me).start()

    qpos = plan_ref[0, me] * tok + lax.broadcasted_iota(jnp.int32, (tok, LANES), 0)
    low = jnp.zeros((tok, LANES), jnp.int32)
    start = jnp.int32(0)
    for i in range(reqs):
        low = jnp.where(start <= qpos, start, low)
        start = start + len_ref[0, i]
    lo_buf[...] = low
    qd_buf[...] = jnp.transpose(
        jnp.broadcast_to(doc_ref[...].astype(jnp.float32), (LANES, tok))
    )

    def attend(g, kref, dref, block, first):
        row = lax.broadcasted_iota(jnp.int32, (tok, tok), 0)
        col = lax.broadcasted_iota(jnp.int32, (tok, tok), 1)
        q_pos = plan_ref[0, me] * tok + row
        k_pos = plan_ref[0, block] * tok + col
        kd = dref[...].astype(jnp.float32)
        qd = wide(qd_buf[...], tok)
        mask = (k_pos <= q_pos) & (k_pos >= wide(lo_buf[...], tok))
        mask = mask & ((kd == qd) | (qd == 0.0))
        keys = kref[:, :HD]
        vals = kref[:, HD:]
        for h in range(gsz):
            hh = g * gsz + h
            s = lax.dot_general(
                q_ref[:, hh * HD : (hh + 1) * HD],
                keys,
                (((1,), (1,)), ((), ())),
                preferred_element_type=jnp.float32,
            )
            z = jnp.where(mask, s * scale, NEG)
            top = jnp.broadcast_to(jnp.max(z, axis=1, keepdims=True), (tok, LANES))
            if not first:
                old = m_buf[hh]
                top = jnp.maximum(top, old)
                alpha = jnp.exp2(old - top)
            p = jnp.exp2(z - wide(top, tok))
            total = p[:, :LANES]
            for i in range(1, tok // LANES):
                total = total + p[:, i * LANES : (i + 1) * LANES]
            update = jnp.dot(
                p.astype(jnp.bfloat16), vals, preferred_element_type=jnp.float32
            )
            m_buf[hh] = top
            if first:
                l_buf[hh] = total
                acc_buf[hh] = update
            else:
                l_buf[hh] = l_buf[hh] * alpha + total
                acc_buf[hh] = acc_buf[hh] * alpha + update

    for g in range(kvh):
        attend(g, kv_ref.at[g], doc_ref, me, True)

    def step_body(step, carry):
        blocks = (me - 1 - step, me + 1 + step)
        arrives = (blocks[0] >= 0, blocks[1] < n)
        for g in range(kvh):
            for way in range(2):
                block = blocks[way]

                @pl.when(arrives[way])
                def _(g=g, way=way, block=block):
                    if g == 0:
                        doc_copy(way, step, dbuf.at[block], block).wait_recv()
                    kv_copy(way, step, g, kvbuf.at[block, g], block).wait_recv()

                    @pl.when(can[way])
                    def _():
                        if g == 0:
                            doc_copy(way, step + 1, dbuf.at[block], block).start()
                        kv_copy(way, step + 1, g, kvbuf.at[block, g], block).start()

            for way in range(2):
                block = blocks[way]

                @pl.when(arrives[way])
                def _(g=g, block=block):
                    attend(g, kvbuf.at[block, g], dbuf.at[block], block, False)

            @pl.when(step == n - 2)
            def _(g=g):
                finish(g)

        return carry

    def att_copy(k, g, half):
        view = att.at[d, pl.ds(half * hrows, hrows), pl.ds(g * gcols, gcols)]
        return pltpu.make_async_remote_copy(
            src_ref=view,
            dst_ref=view,
            send_sem=att_send.at[k - 1, g, half],
            recv_sem=att_recv.at[k - 1, g, half],
            device_id={"dp": lax.rem(d + k, rows)},
            device_id_type=MESH,
        )

    def finish(g):
        for half in range(halves):
            span = pl.ds(half * hrows, hrows)
            for h in range(gsz):
                hh = g * gsz + h
                total = jnp.sum(l_buf[hh, span, :], axis=1, keepdims=True)
                att[d, span, hh * HD : (hh + 1) * HD] = (
                    acc_buf[hh, span, :] / total
                ).astype(jnp.bfloat16)
            for k in range(1, rows):
                att_copy(k, g, half).start()

    lax.fori_loop(0, n - 1, step_body, 0)
    w_copy.wait()

    def part_copy(k, u):
        return pltpu.make_async_remote_copy(
            src_ref=part.at[k, u],
            dst_ref=prec.at[k, u],
            send_sem=part_send.at[k, u],
            recv_sem=part_recv.at[k, u],
            device_id={"tp": other},
            device_id_type=MESH,
        )

    home = d // per_half
    place = lax.rem(d, per_half)

    def out_view(u, spot):
        half = u // chunks
        c = u % chunks
        return out_hbm.at[
            pl.ds(half * hrows, hrows),
            pl.ds(pl.multiple_of(spot * cols + c * ccols, LANES), ccols),
        ]

    def fin_copy(k, u, spot):
        return pltpu.make_async_remote_copy(
            src_ref=fin.at[k, u],
            dst_ref=out_view(u, spot),
            send_sem=fin_send.at[k, u],
            recv_sem=fin_recv.at[spot, u],
            device_id={"dp": lax.rem(d + k, rows), "tp": home},
            device_id_type=MESH,
        )

    def loc_copy(u):
        return pltpu.make_async_copy(fin.at[0, u], out_view(u, place), loc_sem.at[u])

    def keeps(k):
        return lax.rem(lax.rem(d + k, rows), cores) == t

    def multiply(k, u):
        half = u // chunks
        c = u % chunks
        a = att[lax.rem(d + k, rows), half * hrows : (half + 1) * hrows, :]
        part[k, u] = jnp.dot(
            a,
            w_buf[:, c * ccols : (c + 1) * ccols],
            preferred_element_type=jnp.float32,
        ).astype(jnp.bfloat16)

        @pl.when(jnp.logical_not(keeps(k)))
        def _():
            part_copy(k, u).start()

    def settle(k, u):
        @pl.when(keeps(k))
        def _():
            part_copy(k, u).wait_recv()
            fin[k, u] = (
                part[k, u].astype(jnp.float32) + prec[k, u].astype(jnp.float32)
            ).astype(jnp.bfloat16)
            if k == 0:

                @pl.when(home == t)
                def _():
                    loc_copy(u).start()

                @pl.when(home != t)
                def _():
                    fin_copy(k, u, place).start()
            else:
                fin_copy(k, u, place).start()

    for k in range(rows):
        for half in range(halves):
            if k > 0:
                for g in range(kvh):
                    att_copy(k, g, half).wait_recv()
            for c in range(chunks):
                u = half * chunks + c
                multiply(k, u)
                if c > 0:
                    settle(k, u - 1)
            settle(k, half * chunks + chunks - 1)

    for spot in range(per_half):
        source = t * per_half + spot
        local = (source == d) & (lax.rem(d, cores) == t)

        @pl.when(jnp.logical_not(local))
        def _(spot=spot):
            for u in range(halves * chunks):
                fin_copy(0, u, spot).wait_recv()

        @pl.when(local)
        def _():
            for u in range(halves * chunks):
                loc_copy(u).wait()

    for k in range(rows):

        @pl.when(keeps(k))
        def _(k=k):
            for u in range(halves * chunks):
                if k == 0:

                    @pl.when(home != t)
                    def _(u=u):
                        fin_copy(k, u, place).wait_send()
                else:
                    fin_copy(k, u, place).wait_send()

        @pl.when(jnp.logical_not(keeps(k)))
        def _(k=k):
            for u in range(halves * chunks):
                part_copy(k, u).wait_send()

    for k in range(1, rows):
        for g in range(kvh):
            for half in range(halves):
                att_copy(k, g, half).wait_send()

    def drain(step, carry):
        blocks = (me - step, me + step)
        sent = ((blocks[0] >= 0) & can[0], (blocks[1] < n) & can[1])
        for way in range(2):

            @pl.when(sent[way])
            def _(way=way):
                doc_copy(way, step, dbuf.at[blocks[way]], blocks[way]).wait_send()
                for g in range(kvh):
                    kv_copy(
                        way, step, g, kvbuf.at[blocks[way], g], blocks[way]
                    ).wait_send()

        return carry

    lax.fori_loop(0, n - 1, drain, 0)


def per_device(n, rows, cores, queries, keyvals, doc_ids, plan, lengths, out_weight):
    tok = queries.shape[1]
    kvh = keyvals.shape[3] // HD
    heads = queries.shape[2] // HD
    gsz = heads // kvh
    reqs = lengths.shape[1]
    width = queries.shape[2]
    cols = out_weight.shape[1]
    halves = 2
    chunks = 4
    units = halves * chunks
    cfg = (n, rows, cores, tok, kvh, gsz, reqs, cols, halves, chunks)
    kv = (
        keyvals[0]
        .reshape(tok, 2, kvh, HD)
        .transpose(2, 0, 1, 3)
        .reshape(kvh, tok, 2 * HD)
    )
    tile = (rows, units, tok // halves, cols // chunks)
    vmem = pl.BlockSpec(memory_space=pltpu.VMEM)
    smem = pl.BlockSpec(memory_space=pltpu.SMEM)
    anym = pl.BlockSpec(memory_space=pl.ANY)
    dma = pltpu.SemaphoreType.DMA
    out = pl.pallas_call(
        functools.partial(kernel, cfg),
        out_shape=jax.ShapeDtypeStruct((tok, cols * (rows // cores)), jnp.bfloat16),
        in_specs=[smem, smem, vmem, vmem, vmem, anym],
        out_specs=anym,
        scratch_shapes=[
            pltpu.VMEM((n, kvh, tok, 2 * HD), jnp.bfloat16),
            pltpu.VMEM((n, 1, tok), jnp.int32),
            pltpu.VMEM((tok, LANES), jnp.int32),
            pltpu.VMEM((tok, LANES), jnp.float32),
            pltpu.VMEM((heads, tok, LANES), jnp.float32),
            pltpu.VMEM((heads, tok, LANES), jnp.float32),
            pltpu.VMEM((heads, tok, HD), jnp.float32),
            pltpu.VMEM((rows, tok, width), jnp.bfloat16),
            pltpu.VMEM(out_weight.shape, jnp.bfloat16),
            pltpu.VMEM(tile, jnp.bfloat16),
            pltpu.VMEM(tile, jnp.bfloat16),
            pltpu.VMEM(tile, jnp.bfloat16),
            dma,
            dma((2, n - 1, kvh)),
            dma((2, n - 1, kvh)),
            dma((2, n - 1)),
            dma((2, n - 1)),
            dma((rows - 1, kvh, halves)),
            dma((rows - 1, kvh, halves)),
            dma((rows, units)),
            dma((rows, units)),
            dma((rows, units)),
            dma((rows // cores, units)),
            dma((units,)),
        ],
        compiler_params=pltpu.CompilerParams(
            collective_id=0, has_side_effects=True, vmem_limit_bytes=60 * 1024 * 1024
        ),
        name="fused",
    )(plan, lengths, queries[0], kv, doc_ids, out_weight)
    return out[None]


def solution(mesh):
    placed = (
        P(("groups", "dp"), "ctx", "tp"),
        P(("groups", "dp"), "ctx", None, "tp"),
        P(("groups", "dp"), "ctx"),
        P(("groups", "dp"), None),
        P(("groups", "dp"), None),
        P("tp", "dp"),
    )
    sizes = mesh.shape
    return jax.shard_map(
        functools.partial(per_device, sizes["ctx"], sizes["dp"], sizes["tp"]),
        mesh=mesh,
        in_specs=placed,
        out_specs=P(("groups", "dp"), "ctx", "tp"),
        check_vma=False,
    )
```

```python
import functools
import math

import jax
import jax.numpy as jnp
from jax import lax
from jax.experimental import pallas as pl
from jax.experimental.pallas import tpu as pltpu
from jax.sharding import PartitionSpec as P

HD = 128
LANES = 128
MESH = pl.DeviceIdType.MESH
NEG = -1e30


def wide(x, width):
    return jnp.concatenate([x] * (width // LANES), axis=1) if width > LANES else x


def kernel(
    cfg,
    plan_ref,
    len_ref,
    q_ref,
    kv_ref,
    doc_ref,
    w_hbm,
    out_ref,
    kvbuf,
    dbuf,
    lo_buf,
    qd_buf,
    m_buf,
    l_buf,
    acc_buf,
    att,
    w_buf,
    part,
    prec,
    fin,
    w_sem,
    kv_send,
    kv_recv,
    doc_send,
    doc_recv,
    att_send,
    att_recv,
    part_send,
    part_recv,
    fin_send,
    fin_recv,
    loc_sem,
):
    n, rows, cores, tok, kvh, gsz, reqs, cols, halves, chunks = cfg
    me = lax.axis_index("ctx")
    d = lax.axis_index("dp")
    t = lax.axis_index("tp")
    other = 1 - t
    hrows = tok // halves
    ccols = cols // chunks
    gcols = gsz * HD
    per_half = rows // cores
    scale = HD ** (-0.5) * math.log2(math.e)

    w_copy = pltpu.make_async_copy(w_hbm, w_buf, w_sem)
    w_copy.start()

    barrier = pltpu.get_barrier_semaphore()

    @pl.when(me > 0)
    def _():
        pl.semaphore_signal(barrier, inc=1, device_id={"ctx": me - 1}, device_id_type=MESH)

    @pl.when(me < n - 1)
    def _():
        pl.semaphore_signal(barrier, inc=1, device_id={"ctx": me + 1}, device_id_type=MESH)

    for k in range(rows):
        for c in range(cores):
            if k == 0 and c == 0:
                continue
            pl.semaphore_signal(
                barrier,
                inc=1,
                device_id={"dp": lax.rem(d + k, rows), "tp": lax.rem(t + c, cores)},
                device_id_type=MESH,
            )
    pick_row = lax.broadcasted_iota(jnp.int32, (tok, 2 * tok), 0)
    pick_col = lax.broadcasted_iota(jnp.int32, (tok, 2 * tok), 1)
    for which in range(2):
        pick = (pick_col == 2 * pick_row + which).astype(jnp.bfloat16)
        kvbuf[me, which] = jnp.dot(
            pick, kv_ref[...], preferred_element_type=jnp.float32
        ).astype(jnp.bfloat16)

    ends = (me > 0).astype(jnp.int32) + (me < n - 1).astype(jnp.int32)
    pl.semaphore_wait(barrier, rows * cores - 1 + ends)

    def lane(g):
        return pl.ds(g * HD, HD)

    def kv_copy(way, step, g, which, src, block):
        return pltpu.make_async_remote_copy(
            src_ref=src.at[which, :, lane(g)],
            dst_ref=kvbuf.at[block, which, :, lane(g)],
            send_sem=kv_send.at[way, step, g, which],
            recv_sem=kv_recv.at[way, step, g, which],
            device_id={"ctx": me + 1 if way == 0 else me - 1},
            device_id_type=MESH,
        )

    def doc_copy(way, step, src, block):
        return pltpu.make_async_remote_copy(
            src_ref=src,
            dst_ref=dbuf.at[block],
            send_sem=doc_send.at[way, step],
            recv_sem=doc_recv.at[way, step],
            device_id={"ctx": me + 1 if way == 0 else me - 1},
            device_id_type=MESH,
        )

    can = (me < n - 1, me > 0)
    for way in range(2):

        @pl.when(can[way])
        def _(way=way):
            doc_copy(way, 0, doc_ref, me).start()
            for which in range(2):
                kv_copy(way, 0, 0, which, kvbuf.at[me], me).start()
            for g in range(1, kvh):
                kv_copy(way, 0, g, 0, kvbuf.at[me], me).start()

    qpos = plan_ref[0, me] * tok + lax.broadcasted_iota(jnp.int32, (tok, LANES), 0)
    low = jnp.zeros((tok, LANES), jnp.int32)
    start = jnp.int32(0)
    for i in range(reqs):
        low = jnp.where(start <= qpos, start, low)
        start = start + len_ref[0, i]
    lo_buf[...] = low
    qd_buf[...] = jnp.transpose(
        jnp.broadcast_to(doc_ref[...].astype(jnp.float32), (LANES, tok))
    )

    def attend(g, kref, dref, block, first):
        row = lax.broadcasted_iota(jnp.int32, (tok, tok), 0)
        col = lax.broadcasted_iota(jnp.int32, (tok, tok), 1)
        q_pos = plan_ref[0, me] * tok + row
        k_pos = plan_ref[0, block] * tok + col
        kd = dref[...].astype(jnp.float32)
        qd = wide(qd_buf[...], tok)
        mask = (k_pos <= q_pos) & (k_pos >= wide(lo_buf[...], tok))
        mask = mask & ((kd == qd) | (qd == 0.0))
        keys = kref[0, :, g * HD : (g + 1) * HD]
        vals = kref[1, :, g * HD : (g + 1) * HD]
        for h in range(gsz):
            hh = g * gsz + h
            s = lax.dot_general(
                q_ref[:, hh * HD : (hh + 1) * HD],
                keys,
                (((1,), (1,)), ((), ())),
                preferred_element_type=jnp.float32,
            )
            z = jnp.where(mask, s * scale, NEG)
            top = jnp.broadcast_to(jnp.max(z, axis=1, keepdims=True), (tok, LANES))
            if not first:
                old = m_buf[hh]
                top = jnp.maximum(top, old)
                alpha = jnp.exp2(old - top)
            p = jnp.exp2(z - wide(top, tok))
            total = p[:, :LANES]
            for i in range(1, tok // LANES):
                total = total + p[:, i * LANES : (i + 1) * LANES]
            update = jnp.dot(
                p.astype(jnp.bfloat16), vals, preferred_element_type=jnp.float32
            )
            m_buf[hh] = top
            if first:
                l_buf[hh] = total
                acc_buf[hh] = update
            else:
                l_buf[hh] = l_buf[hh] * alpha + total
                acc_buf[hh] = acc_buf[hh] * alpha + update

    def receive(g, step):
        blocks = (me - 1 - step, me + 1 + step)
        arrives = (blocks[0] >= 0, blocks[1] < n)
        for way in range(2):
            block = blocks[way]

            @pl.when(arrives[way])
            def _(way=way, block=block):
                if g == 0:
                    doc_copy(way, step, dbuf.at[block], block).wait_recv()
                for which in range(2):
                    kv_copy(way, step, g, which, kvbuf.at[block], block).wait_recv()

                @pl.when(can[way])
                def _():
                    if g == 0:
                        doc_copy(way, step + 1, dbuf.at[block], block).start()
                    for which in range(2):
                        kv_copy(way, step + 1, g, which, kvbuf.at[block], block).start()

    def absorb(g, step):
        blocks = (me - 1 - step, me + 1 + step)
        arrives = (blocks[0] >= 0, blocks[1] < n)
        for way in range(2):
            block = blocks[way]

            @pl.when(arrives[way])
            def _(block=block):
                attend(g, kvbuf.at[block], dbuf.at[block], block, False)

    def att_copy(k, g, half):
        view = att.at[d, pl.ds(half * hrows, hrows), pl.ds(g * gcols, gcols)]
        return pltpu.make_async_remote_copy(
            src_ref=view,
            dst_ref=view,
            send_sem=att_send.at[k - 1, g, half],
            recv_sem=att_recv.at[k - 1, g, half],
            device_id={"dp": lax.rem(d + k, rows)},
            device_id_type=MESH,
        )

    def finish(g):
        for half in range(halves):
            span = pl.ds(half * hrows, hrows)
            for h in range(gsz):
                hh = g * gsz + h
                total = jnp.sum(l_buf[hh, span, :], axis=1, keepdims=True)
                att[d, span, hh * HD : (hh + 1) * HD] = (
                    acc_buf[hh, span, :] / total
                ).astype(jnp.bfloat16)
            for k in range(1, rows):
                att_copy(k, g, half).start()

    for g in range(kvh):
        attend(g, kvbuf.at[me], doc_ref, me, True)

    def step_body(step, carry):
        @pl.when(step < n - 1)
        def _():
            receive(0, step)

        @pl.when(step == 0)
        def _():
            for way in range(2):

                @pl.when(can[way])
                def _(way=way):
                    for g in range(1, kvh):
                        kv_copy(way, 0, g, 1, kvbuf.at[me], me).start()

        @pl.when(step < n - 1)
        def _():
            absorb(0, step)

        @pl.when(step == n - 2)
        def _():
            finish(0)

        @pl.when(step > 0)
        def _():
            for g in range(1, kvh):
                receive(g, step - 1)
                absorb(g, step - 1)

        return carry

    lax.fori_loop(0, n, step_body, 0)
    for g in range(1, kvh):
        finish(g)
    w_copy.wait()

    def part_copy(k, u):
        return pltpu.make_async_remote_copy(
            src_ref=part.at[k, u],
            dst_ref=prec.at[k, u],
            send_sem=part_send.at[k, u],
            recv_sem=part_recv.at[k, u],
            device_id={"tp": other},
            device_id_type=MESH,
        )

    home = d // per_half
    place = lax.rem(d, per_half)

    def out_view(u, spot):
        half = u // chunks
        c = u % chunks
        return out_ref.at[
            pl.ds(half * hrows, hrows),
            pl.ds(pl.multiple_of(spot * cols + c * ccols, LANES), ccols),
        ]

    def fin_copy(k, u, spot):
        return pltpu.make_async_remote_copy(
            src_ref=fin.at[k, u],
            dst_ref=out_view(u, spot),
            send_sem=fin_send.at[k, u],
            recv_sem=fin_recv.at[spot, u],
            device_id={"dp": lax.rem(d + k, rows), "tp": home},
            device_id_type=MESH,
        )

    def loc_copy(u):
        return pltpu.make_async_copy(fin.at[0, u], out_view(u, place), loc_sem.at[u])

    def keeps(k):
        return lax.rem(lax.rem(d + k, rows), cores) == t

    def multiply(k, u):
        half = u // chunks
        c = u % chunks
        a = att[lax.rem(d + k, rows), half * hrows : (half + 1) * hrows, :]
        part[k, u] = jnp.dot(
            a,
            w_buf[:, c * ccols : (c + 1) * ccols],
            preferred_element_type=jnp.float32,
        ).astype(jnp.bfloat16)

        @pl.when(jnp.logical_not(keeps(k)))
        def _():
            part_copy(k, u).start()

    def settle(k, u):
        @pl.when(keeps(k))
        def _():
            part_copy(k, u).wait_recv()
            fin[k, u] = (
                part[k, u].astype(jnp.float32) + prec[k, u].astype(jnp.float32)
            ).astype(jnp.bfloat16)
            if k == 0:

                @pl.when(home == t)
                def _():
                    loc_copy(u).start()

                @pl.when(home != t)
                def _():
                    fin_copy(k, u, place).start()
            else:
                fin_copy(k, u, place).start()

    for k in range(rows):
        for half in range(halves):
            if k > 0:
                for g in range(kvh):
                    att_copy(k, g, half).wait_recv()
            for c in range(chunks):
                u = half * chunks + c
                multiply(k, u)
                if c > 0:
                    settle(k, u - 1)
            settle(k, half * chunks + chunks - 1)

    for spot in range(per_half):
        source = t * per_half + spot
        local = (source == d) & (lax.rem(d, cores) == t)

        @pl.when(jnp.logical_not(local))
        def _(spot=spot):
            for u in range(halves * chunks):
                fin_copy(0, u, spot).wait_recv()

        @pl.when(local)
        def _():
            for u in range(halves * chunks):
                loc_copy(u).wait()

    for k in range(rows):

        @pl.when(keeps(k))
        def _(k=k):
            for u in range(halves * chunks):
                if k == 0:

                    @pl.when(home != t)
                    def _(u=u):
                        fin_copy(k, u, place).wait_send()
                else:
                    fin_copy(k, u, place).wait_send()

        @pl.when(jnp.logical_not(keeps(k)))
        def _(k=k):
            for u in range(halves * chunks):
                part_copy(k, u).wait_send()

    for k in range(1, rows):
        for g in range(kvh):
            for half in range(halves):
                att_copy(k, g, half).wait_send()

    def drain(step, carry):
        blocks = (me - step, me + step)
        sent = ((blocks[0] >= 0) & can[0], (blocks[1] < n) & can[1])
        for way in range(2):

            @pl.when(sent[way])
            def _(way=way):
                doc_copy(way, step, dbuf.at[blocks[way]], blocks[way]).wait_send()
                for g in range(kvh):
                    for which in range(2):
                        kv_copy(
                            way, step, g, which, kvbuf.at[blocks[way]], blocks[way]
                        ).wait_send()

        return carry

    lax.fori_loop(0, n - 1, drain, 0)


def per_device(n, rows, cores, queries, keyvals, doc_ids, plan, lengths, out_weight):
    tok = queries.shape[1]
    kvh = keyvals.shape[3] // HD
    heads = queries.shape[2] // HD
    gsz = heads // kvh
    reqs = lengths.shape[1]
    width = queries.shape[2]
    cols = out_weight.shape[1]
    halves = 2
    chunks = 4
    units = halves * chunks
    cfg = (n, rows, cores, tok, kvh, gsz, reqs, cols, halves, chunks)
    kv = keyvals[0].reshape(2 * tok, kvh * HD)
    tile = (rows, units, tok // halves, cols // chunks)
    vmem = pl.BlockSpec(memory_space=pltpu.VMEM)
    smem = pl.BlockSpec(memory_space=pltpu.SMEM)
    hbm = pl.BlockSpec(memory_space=pltpu.HBM)
    dma = pltpu.SemaphoreType.DMA
    out = pl.pallas_call(
        functools.partial(kernel, cfg),
        out_shape=jax.ShapeDtypeStruct((tok, cols * (rows // cores)), jnp.bfloat16),
        in_specs=[smem, smem, vmem, vmem, vmem, hbm],
        out_specs=vmem,
        scratch_shapes=[
            pltpu.VMEM((n, 2, tok, kvh * HD), jnp.bfloat16),
            pltpu.VMEM((n, 1, tok), jnp.int32),
            pltpu.VMEM((tok, LANES), jnp.int32),
            pltpu.VMEM((tok, LANES), jnp.float32),
            pltpu.VMEM((heads, tok, LANES), jnp.float32),
            pltpu.VMEM((heads, tok, LANES), jnp.float32),
            pltpu.VMEM((heads, tok, HD), jnp.float32),
            pltpu.VMEM((rows, tok, width), jnp.bfloat16),
            pltpu.VMEM(out_weight.shape, jnp.bfloat16),
            pltpu.VMEM(tile, jnp.bfloat16),
            pltpu.VMEM(tile, jnp.bfloat16),
            pltpu.VMEM(tile, jnp.bfloat16),
            dma,
            dma((2, n - 1, kvh, 2)),
            dma((2, n - 1, kvh, 2)),
            dma((2, n - 1)),
            dma((2, n - 1)),
            dma((rows - 1, kvh, halves)),
            dma((rows - 1, kvh, halves)),
            dma((rows, units)),
            dma((rows, units)),
            dma((rows, units)),
            dma((rows // cores, units)),
            dma((units,)),
        ],
        compiler_params=pltpu.CompilerParams(
            collective_id=0, has_side_effects=True, vmem_limit_bytes=61 * 1024 * 1024
        ),
        name="fused",
    )(plan, lengths, queries[0], kv, doc_ids, out_weight)
    return out[None]


def solution(mesh):
    placed = (
        P(("groups", "dp"), "ctx", "tp"),
        P(("groups", "dp"), "ctx", None, "tp"),
        P(("groups", "dp"), "ctx"),
        P(("groups", "dp"), None),
        P(("groups", "dp"), None),
        P("tp", "dp"),
    )
    sizes = mesh.shape
    return jax.shard_map(
        functools.partial(per_device, sizes["ctx"], sizes["dp"], sizes["tp"]),
        mesh=mesh,
        in_specs=placed,
        out_specs=P(("groups", "dp"), "ctx", "tp"),
        check_vma=False,
    )
```

```python
import functools
import math

import jax
import jax.numpy as jnp
from jax import lax
from jax.experimental import pallas as pl
from jax.experimental.pallas import tpu as pltpu
from jax.sharding import PartitionSpec as P

HD = 128
LANES = 128
MESH = pl.DeviceIdType.MESH
NEG = -1e30


def wide(x, width):
    return jnp.concatenate([x] * (width // LANES), axis=1) if width > LANES else x


def kernel(
    cfg,
    plan_ref,
    len_ref,
    q_ref,
    kv_ref,
    doc_ref,
    w_hbm,
    out_ref,
    kvbuf,
    dbuf,
    lo_buf,
    qd_buf,
    m_buf,
    l_buf,
    acc_buf,
    att,
    w_buf,
    part,
    prec,
    fin,
    far_w,
    far_part,
    far_prec,
    far_fin,
    w_sem,
    kv_send,
    kv_recv,
    doc_send,
    doc_recv,
    att_send,
    att_recv,
    part_send,
    part_recv,
    fin_send,
    fin_recv,
    loc_sem,
    far_send,
    far_recv,
    swap_send,
    swap_recv,
    fp_send,
    fp_recv,
    far_loc,
):
    n, rows, cores, packs, tok, kvh, gsz, reqs, cols, halves, chunks = cfg
    me = lax.axis_index("ctx")
    d = lax.axis_index("dp")
    t = lax.axis_index("tp")
    gy = lax.axis_index("groups")
    kept = chunks - packs
    other = 1 - t
    hrows = tok // halves
    ccols = cols // chunks
    gcols = gsz * HD
    per_half = rows // cores
    scale = HD ** (-0.5) * math.log2(math.e)

    w_copy = pltpu.make_async_copy(w_hbm, w_buf, w_sem)
    w_copy.start()

    barrier = pltpu.get_barrier_semaphore()

    @pl.when(me > 0)
    def _():
        pl.semaphore_signal(barrier, inc=1, device_id={"ctx": me - 1}, device_id_type=MESH)

    @pl.when(me < n - 1)
    def _():
        pl.semaphore_signal(barrier, inc=1, device_id={"ctx": me + 1}, device_id_type=MESH)

    for k in range(rows):
        for c in range(cores):
            if k == 0 and c == 0:
                continue
            pl.semaphore_signal(
                barrier,
                inc=1,
                device_id={"dp": lax.rem(d + k, rows), "tp": lax.rem(t + c, cores)},
                device_id_type=MESH,
            )
    for j in range(1, packs):
        pl.semaphore_signal(
            barrier,
            inc=1,
            device_id={"groups": lax.rem(gy + j, packs)},
            device_id_type=MESH,
        )
    pick_row = lax.broadcasted_iota(jnp.int32, (tok, 2 * tok), 0)
    pick_col = lax.broadcasted_iota(jnp.int32, (tok, 2 * tok), 1)
    for which in range(2):
        pick = (pick_col == 2 * pick_row + which).astype(jnp.bfloat16)
        kvbuf[me, which] = jnp.dot(
            pick, kv_ref[...], preferred_element_type=jnp.float32
        ).astype(jnp.bfloat16)

    ends = (me > 0).astype(jnp.int32) + (me < n - 1).astype(jnp.int32)
    pl.semaphore_wait(barrier, rows * cores - 1 + packs - 1 + ends)

    def lane(g):
        return pl.ds(g * HD, HD)

    def kv_copy(way, step, g, which, src, block):
        return pltpu.make_async_remote_copy(
            src_ref=src.at[which, :, lane(g)],
            dst_ref=kvbuf.at[block, which, :, lane(g)],
            send_sem=kv_send.at[way, step, g, which],
            recv_sem=kv_recv.at[way, step, g, which],
            device_id={"ctx": me + 1 if way == 0 else me - 1},
            device_id_type=MESH,
        )

    def doc_copy(way, step, src, block):
        return pltpu.make_async_remote_copy(
            src_ref=src,
            dst_ref=dbuf.at[block],
            send_sem=doc_send.at[way, step],
            recv_sem=doc_recv.at[way, step],
            device_id={"ctx": me + 1 if way == 0 else me - 1},
            device_id_type=MESH,
        )

    can = (me < n - 1, me > 0)
    for way in range(2):

        @pl.when(can[way])
        def _(way=way):
            doc_copy(way, 0, doc_ref, me).start()
            for which in range(2):
                kv_copy(way, 0, 0, which, kvbuf.at[me], me).start()
            for g in range(1, kvh):
                kv_copy(way, 0, g, 0, kvbuf.at[me], me).start()

    def far_copy(k):
        start = pl.multiple_of((kept + gy) * ccols, LANES)
        return pltpu.make_async_remote_copy(
            src_ref=w_hbm.at[:, pl.ds(start, ccols)],
            dst_ref=far_w.at[k - 1, gy],
            send_sem=far_send.at[k - 1],
            recv_sem=far_recv.at[k - 1],
            device_id={"dp": lax.rem(d + k, rows)},
            device_id_type=MESH,
        )

    def swap_copy(k, j, pack):
        return pltpu.make_async_remote_copy(
            src_ref=far_w.at[k - 1, pack],
            dst_ref=far_w.at[k - 1, pack],
            send_sem=swap_send.at[k - 1, j - 1],
            recv_sem=swap_recv.at[k - 1, j - 1],
            device_id={"groups": lax.rem(gy + j, packs)},
            device_id_type=MESH,
        )

    for k in range(1, rows):
        far_copy(k).start()

    qpos = plan_ref[0, me] * tok + lax.broadcasted_iota(jnp.int32, (tok, LANES), 0)
    low = jnp.zeros((tok, LANES), jnp.int32)
    start = jnp.int32(0)
    for i in range(reqs):
        low = jnp.where(start <= qpos, start, low)
        start = start + len_ref[0, i]
    lo_buf[...] = low
    qd_buf[...] = jnp.transpose(
        jnp.broadcast_to(doc_ref[...].astype(jnp.float32), (LANES, tok))
    )

    def attend(g, kref, dref, block, first):
        row = lax.broadcasted_iota(jnp.int32, (tok, tok), 0)
        col = lax.broadcasted_iota(jnp.int32, (tok, tok), 1)
        q_pos = plan_ref[0, me] * tok + row
        k_pos = plan_ref[0, block] * tok + col
        kd = dref[...].astype(jnp.float32)
        qd = wide(qd_buf[...], tok)
        mask = (k_pos <= q_pos) & (k_pos >= wide(lo_buf[...], tok))
        mask = mask & ((kd == qd) | (qd == 0.0))
        keys = kref[0, :, g * HD : (g + 1) * HD]
        vals = kref[1, :, g * HD : (g + 1) * HD]
        for h in range(gsz):
            hh = g * gsz + h
            s = lax.dot_general(
                q_ref[:, hh * HD : (hh + 1) * HD],
                keys,
                (((1,), (1,)), ((), ())),
                preferred_element_type=jnp.float32,
            )
            z = jnp.where(mask, s * scale, NEG)
            top = jnp.broadcast_to(jnp.max(z, axis=1, keepdims=True), (tok, LANES))
            if not first:
                old = m_buf[hh]
                top = jnp.maximum(top, old)
                alpha = jnp.exp2(old - top)
            p = jnp.exp2(z - wide(top, tok))
            total = p[:, :LANES]
            for i in range(1, tok // LANES):
                total = total + p[:, i * LANES : (i + 1) * LANES]
            update = jnp.dot(
                p.astype(jnp.bfloat16), vals, preferred_element_type=jnp.float32
            )
            m_buf[hh] = top
            if first:
                l_buf[hh] = total
                acc_buf[hh] = update
            else:
                l_buf[hh] = l_buf[hh] * alpha + total
                acc_buf[hh] = acc_buf[hh] * alpha + update

    def receive(g, step):
        blocks = (me - 1 - step, me + 1 + step)
        arrives = (blocks[0] >= 0, blocks[1] < n)
        for way in range(2):
            block = blocks[way]

            @pl.when(arrives[way])
            def _(way=way, block=block):
                if g == 0:
                    doc_copy(way, step, dbuf.at[block], block).wait_recv()
                for which in range(2):
                    kv_copy(way, step, g, which, kvbuf.at[block], block).wait_recv()

                @pl.when(can[way])
                def _():
                    if g == 0:
                        doc_copy(way, step + 1, dbuf.at[block], block).start()
                    for which in range(2):
                        kv_copy(way, step + 1, g, which, kvbuf.at[block], block).start()

    def absorb(g, step):
        blocks = (me - 1 - step, me + 1 + step)
        arrives = (blocks[0] >= 0, blocks[1] < n)
        for way in range(2):
            block = blocks[way]

            @pl.when(arrives[way])
            def _(block=block):
                attend(g, kvbuf.at[block], dbuf.at[block], block, False)

    def att_copy(k, g, half):
        view = att.at[d, pl.ds(half * hrows, hrows), pl.ds(g * gcols, gcols)]
        return pltpu.make_async_remote_copy(
            src_ref=view,
            dst_ref=view,
            send_sem=att_send.at[k - 1, g, half],
            recv_sem=att_recv.at[k - 1, g, half],
            device_id={"dp": lax.rem(d + k, rows)},
            device_id_type=MESH,
        )

    def finish(g):
        for half in range(halves):
            span = pl.ds(half * hrows, hrows)
            for h in range(gsz):
                hh = g * gsz + h
                total = jnp.sum(l_buf[hh, span, :], axis=1, keepdims=True)
                att[d, span, hh * HD : (hh + 1) * HD] = (
                    acc_buf[hh, span, :] / total
                ).astype(jnp.bfloat16)
            for k in range(1, rows):
                att_copy(k, g, half).start()

    for g in range(kvh):
        attend(g, kvbuf.at[me], doc_ref, me, True)

    def step_body(step, carry):
        @pl.when(step < n - 1)
        def _():
            receive(0, step)

        @pl.when(step == 0)
        def _():
            for way in range(2):

                @pl.when(can[way])
                def _(way=way):
                    for g in range(1, kvh):
                        kv_copy(way, 0, g, 1, kvbuf.at[me], me).start()

        @pl.when(step < n - 1)
        def _():
            absorb(0, step)

        @pl.when(step == n - 2)
        def _():
            finish(0)

        @pl.when(step > 0)
        def _():
            for g in range(1, kvh):
                receive(g, step - 1)
                absorb(g, step - 1)

        return carry

    lax.fori_loop(0, n, step_body, 0)
    for g in range(1, kvh):
        finish(g)
    w_copy.wait()

    def part_copy(k, u):
        return pltpu.make_async_remote_copy(
            src_ref=part.at[k, u],
            dst_ref=prec.at[k, u],
            send_sem=part_send.at[k, u],
            recv_sem=part_recv.at[k, u],
            device_id={"tp": other},
            device_id_type=MESH,
        )

    home = d // per_half
    place = lax.rem(d, per_half)

    def out_view(u, spot):
        half = u // chunks
        c = u % chunks
        return out_ref.at[
            pl.ds(half * hrows, hrows),
            pl.ds(pl.multiple_of(spot * cols + c * ccols, LANES), ccols),
        ]

    def fin_copy(k, u, spot):
        return pltpu.make_async_remote_copy(
            src_ref=fin.at[k, u],
            dst_ref=out_view(u, spot),
            send_sem=fin_send.at[k, u],
            recv_sem=fin_recv.at[spot, u],
            device_id={"dp": lax.rem(d + k, rows), "tp": home},
            device_id_type=MESH,
        )

    def loc_copy(u):
        return pltpu.make_async_copy(fin.at[0, u], out_view(u, place), loc_sem.at[u])

    def keeps(k):
        return lax.rem(lax.rem(d + k, rows), cores) == t

    def multiply(k, u):
        half = u // chunks
        c = u % chunks
        a = att[lax.rem(d + k, rows), half * hrows : (half + 1) * hrows, :]
        part[k, u] = jnp.dot(
            a,
            w_buf[:, c * ccols : (c + 1) * ccols],
            preferred_element_type=jnp.float32,
        ).astype(jnp.bfloat16)

        @pl.when(jnp.logical_not(keeps(k)))
        def _():
            part_copy(k, u).start()

    def settle(k, u):
        @pl.when(keeps(k))
        def _():
            part_copy(k, u).wait_recv()
            fin[k, u] = (
                part[k, u].astype(jnp.float32) + prec[k, u].astype(jnp.float32)
            ).astype(jnp.bfloat16)
            if k == 0:

                @pl.when(home == t)
                def _():
                    loc_copy(u).start()

                @pl.when(home != t)
                def _():
                    fin_copy(k, u, place).start()
            else:
                fin_copy(k, u, place).start()

    def far_home(k):
        source = lax.rem(d - k + rows, rows)
        return source // per_half, lax.rem(source, per_half)

    def far_pack(j):
        return lax.rem(gy - j + packs, packs)

    def far_pcopy(k, j, half):
        return pltpu.make_async_remote_copy(
            src_ref=far_part.at[k - 1, j, half],
            dst_ref=far_prec.at[k - 1, j, half],
            send_sem=fp_send.at[k - 1, j, half],
            recv_sem=fp_recv.at[k - 1, j, half],
            device_id={"tp": other},
            device_id_type=MESH,
        )

    def far_lcopy(k, j, half):
        column = far_home(k)[1] * cols + (kept + far_pack(j)) * ccols
        return pltpu.make_async_copy(
            far_fin.at[k - 1, j, half],
            out_ref.at[
                pl.ds(half * hrows, hrows), pl.ds(pl.multiple_of(column, LANES), ccols)
            ],
            far_loc.at[k - 1, j, half],
        )

    def far_multiply(k, j):
        for half in range(halves):
            far_part[k - 1, j, half] = jnp.dot(
                att[d, half * hrows : (half + 1) * hrows, :],
                far_w[k - 1, far_pack(j)],
                preferred_element_type=jnp.float32,
            ).astype(jnp.bfloat16)

            @pl.when(far_home(k)[0] != t)
            def _(half=half):
                far_pcopy(k, j, half).start()

    def far_settle(k, j):
        @pl.when(far_home(k)[0] == t)
        def _():
            for half in range(halves):
                far_pcopy(k, j, half).wait_recv()
                far_fin[k - 1, j, half] = (
                    far_part[k - 1, j, half].astype(jnp.float32)
                    + far_prec[k - 1, j, half].astype(jnp.float32)
                ).astype(jnp.bfloat16)
                far_lcopy(k, j, half).start()

    for k in range(1, rows):
        far_copy(k).wait_recv()
        for j in range(1, packs):
            swap_copy(k, j, gy).start()

    for k in range(rows):
        limit = chunks if k == 0 else kept
        for half in range(halves):
            if k > 0:
                for g in range(kvh):
                    att_copy(k, g, half).wait_recv()
            for c in range(limit):
                u = half * chunks + c
                multiply(k, u)
                if c > 0:
                    settle(k, u - 1)
            settle(k, half * chunks + limit - 1)
        if k == 0:
            for kk in range(1, rows):
                far_multiply(kk, 0)

    for k in range(1, rows):
        for j in range(1, packs):
            swap_copy(k, j, far_pack(j)).wait_recv()
            far_multiply(k, j)
        for j in range(packs):
            far_settle(k, j)

    own_units = [h * chunks + c for h in range(halves) for c in range(chunks)]
    row_units = [h * chunks + c for h in range(halves) for c in range(kept)]
    for spot in range(per_half):
        source = t * per_half + spot
        near = source == d
        local = near & (lax.rem(d, cores) == t)

        @pl.when(jnp.logical_not(near))
        def _(spot=spot):
            for u in row_units:
                fin_copy(0, u, spot).wait_recv()

        @pl.when(near & jnp.logical_not(local))
        def _(spot=spot):
            for u in own_units:
                fin_copy(0, u, spot).wait_recv()

        @pl.when(local)
        def _():
            for u in own_units:
                loc_copy(u).wait()

    for k in range(rows):

        @pl.when(keeps(k))
        def _(k=k):
            if k == 0:

                @pl.when(home != t)
                def _():
                    for u in own_units:
                        fin_copy(k, u, place).wait_send()
            else:
                for u in row_units:
                    fin_copy(k, u, place).wait_send()

        @pl.when(jnp.logical_not(keeps(k)))
        def _(k=k):
            for u in own_units if k == 0 else row_units:
                part_copy(k, u).wait_send()

    for k in range(1, rows):
        far_copy(k).wait_send()
        for j in range(1, packs):
            swap_copy(k, j, gy).wait_send()

        @pl.when(far_home(k)[0] == t)
        def _(k=k):
            for j in range(packs):
                for half in range(halves):
                    far_lcopy(k, j, half).wait()

        @pl.when(far_home(k)[0] != t)
        def _(k=k):
            for j in range(packs):
                for half in range(halves):
                    far_pcopy(k, j, half).wait_send()

    for k in range(1, rows):
        for g in range(kvh):
            for half in range(halves):
                att_copy(k, g, half).wait_send()

    def drain(step, carry):
        blocks = (me - step, me + step)
        sent = ((blocks[0] >= 0) & can[0], (blocks[1] < n) & can[1])
        for way in range(2):

            @pl.when(sent[way])
            def _(way=way):
                doc_copy(way, step, dbuf.at[blocks[way]], blocks[way]).wait_send()
                for g in range(kvh):
                    for which in range(2):
                        kv_copy(
                            way, step, g, which, kvbuf.at[blocks[way]], blocks[way]
                        ).wait_send()

        return carry

    lax.fori_loop(0, n - 1, drain, 0)


def per_device(n, rows, cores, packs, queries, keyvals, doc_ids, plan, lengths, out_weight):
    tok = queries.shape[1]
    kvh = keyvals.shape[3] // HD
    heads = queries.shape[2] // HD
    gsz = heads // kvh
    reqs = lengths.shape[1]
    width = queries.shape[2]
    cols = out_weight.shape[1]
    halves = 2
    chunks = cols // (2 * LANES)
    units = halves * chunks
    cfg = (n, rows, cores, packs, tok, kvh, gsz, reqs, cols, halves, chunks)
    kv = keyvals[0].reshape(2 * tok, kvh * HD)
    tile = (rows, units, tok // halves, cols // chunks)
    far = (rows - 1, packs, halves, tok // halves, cols // chunks)
    vmem = pl.BlockSpec(memory_space=pltpu.VMEM)
    smem = pl.BlockSpec(memory_space=pltpu.SMEM)
    hbm = pl.BlockSpec(memory_space=pltpu.HBM)
    dma = pltpu.SemaphoreType.DMA
    out = pl.pallas_call(
        functools.partial(kernel, cfg),
        out_shape=jax.ShapeDtypeStruct((tok, cols * (rows // cores)), jnp.bfloat16),
        in_specs=[smem, smem, vmem, vmem, vmem, hbm],
        out_specs=hbm,
        scratch_shapes=[
            pltpu.VMEM((n, 2, tok, kvh * HD), jnp.bfloat16),
            pltpu.VMEM((n, 1, tok), jnp.int32),
            pltpu.VMEM((tok, LANES), jnp.int32),
            pltpu.VMEM((tok, LANES), jnp.float32),
            pltpu.VMEM((heads, tok, LANES), jnp.float32),
            pltpu.VMEM((heads, tok, LANES), jnp.float32),
            pltpu.VMEM((heads, tok, HD), jnp.float32),
            pltpu.VMEM((rows, tok, width), jnp.bfloat16),
            pltpu.VMEM(out_weight.shape, jnp.bfloat16),
            pltpu.VMEM(tile, jnp.bfloat16),
            pltpu.VMEM(tile, jnp.bfloat16),
            pltpu.VMEM(tile, jnp.bfloat16),
            pltpu.VMEM((rows - 1, packs, width, cols // chunks), jnp.bfloat16),
            pltpu.VMEM(far, jnp.bfloat16),
            pltpu.VMEM(far, jnp.bfloat16),
            pltpu.VMEM(far, jnp.bfloat16),
            dma,
            dma((2, n - 1, kvh, 2)),
            dma((2, n - 1, kvh, 2)),
            dma((2, n - 1)),
            dma((2, n - 1)),
            dma((rows - 1, kvh, halves)),
            dma((rows - 1, kvh, halves)),
            dma((rows, units)),
            dma((rows, units)),
            dma((rows, units)),
            dma((rows // cores, units)),
            dma((units,)),
            dma((rows - 1,)),
            dma((rows - 1,)),
            dma((rows - 1, packs - 1)),
            dma((rows - 1, packs - 1)),
            dma((rows - 1, packs, halves)),
            dma((rows - 1, packs, halves)),
            dma((rows - 1, packs, halves)),
        ],
        compiler_params=pltpu.CompilerParams(
            collective_id=0, has_side_effects=True, vmem_limit_bytes=61 * 1024 * 1024
        ),
        name="fused",
    )(plan, lengths, queries[0], kv, doc_ids, out_weight)
    return out[None]


def solution(mesh):
    placed = (
        P(("groups", "dp"), "ctx", "tp"),
        P(("groups", "dp"), "ctx", None, "tp"),
        P(("groups", "dp"), "ctx"),
        P(("groups", "dp"), None),
        P(("groups", "dp"), None),
        P("tp", "dp"),
    )
    sizes = mesh.shape
    return jax.shard_map(
        functools.partial(per_device, sizes["ctx"], sizes["dp"], sizes["tp"], sizes["groups"]),
        mesh=mesh,
        in_specs=placed,
        out_specs=P(("groups", "dp"), "ctx", "tp"),
        check_vma=False,
    )
```
